32 devices in a mesh: rep: 2 (over x), seq: 16 (over z, y, core).
Axes of the slice: x: 2, y: 2, z: 4, core: 2. Of those that a mesh axis runs over, the one named last changes fastest.
Arguments:
- keys: bfloat16 [2048, 5120], P(('rep', 'seq')), parts along dimension 0, may hold values from -36 to 36
- values: bfloat16 [2048, 5120], P(('rep', 'seq')), parts along dimension 0, may hold values from -6 to 6
- queries: bfloat16 [2, 1024, 5120], P(None, ('rep', 'seq')), parts along dimension 1, may hold values from -6 to 6
Outputs:
- attended: bfloat16 [2, 1024, 5120], P(None, ('rep', 'seq')), parts along dimension 1
The draws below stay inside these ranges and needn't reach their ends.
There are 2 independent parts, one for each index of `rep`. The reference program is written for one: setup_inputs(seed, part) draws one part's arguments, and reference() takes and returns one part's arrays. A program takes and returns all parts, laid end to end along the dimension named above; each array names one. Nothing has to cross between parts.
All inputs are finite; a program needn't handle non-finite values.
Results may differ from the reference program's by a relative error of at most 0.0038.
Values may be sent and summed in bfloat16 or wider, within the bound.
A program may use at most 128 MiB of HBM per device.

```python
import math
import jax
import jax.numpy as jnp
from jax import lax

D = 5120
HEADS = 40
HEAD_DIM = 128
CTX_DEV = 64
QUERY_TOKENS = 512
LAYERS = 2
CONTEXT = 1024


key_floor = 2.0


aligned_gain = 0.8


def shared_pattern(key):
    return jnp.sign(jax.random.normal(jax.random.fold_in(key, 41), (D,), jnp.float32))


def drawn_positions(key):
    block_count = CONTEXT // CTX_DEV
    offsets = jax.random.randint(jax.random.fold_in(key, 42), (block_count,), 4, CTX_DEV)
    return jnp.arange(block_count, dtype=jnp.int32) * CTX_DEV + offsets


def draw_keys(key, part):
    row_scale = jnp.exp(jax.random.uniform(jax.random.fold_in(key, 22), (CONTEXT, 1), jnp.float32, math.log(2.5), math.log(6.0)))
    base = jnp.clip(jax.random.normal(jax.random.fold_in(key, 21), (CONTEXT, D), jnp.float32), -6.0, 6.0)
    drawn = base * row_scale
    positions = drawn_positions(key)
    floor_rows = jnp.broadcast_to(key_floor * shared_pattern(key)[None], (positions.shape[0], D))
    drawn = drawn.at[positions].set(floor_rows)
    return drawn.astype(jnp.bfloat16)


def draw_queries(key, part):
    aligned = jnp.arange(QUERY_TOKENS, dtype=jnp.int32) % 4 == 2
    noise = jax.random.normal(jax.random.fold_in(key, 32), (LAYERS, QUERY_TOKENS, D), jnp.float32)
    matched = jnp.clip(aligned_gain * shared_pattern(key)[None, None] + 0.25 * noise, -6.0, 6.0)
    drawn = jnp.clip(jax.random.normal(jax.random.fold_in(key, 31), (LAYERS, QUERY_TOKENS, D), jnp.float32), -6.0, 6.0)
    drawn = jnp.where(aligned[None, :, None], matched, drawn)
    return drawn.astype(jnp.bfloat16)


def level_of(key, extent, cuts, least, top_value):
    def one(dim, shards_of):
        steps = jax.random.uniform(jax.random.fold_in(jax.random.fold_in(key, 6), dim), (shards_of,), jnp.float32, least / len(cuts), top_value / len(cuts))
        return jnp.repeat(jnp.exp(steps), extent[dim] // shards_of).reshape((-1,) + (1,) * (len(extent) - dim - 1))

    gain = one(*cuts[0])
    for cut in cuts[1:]:
        gain = gain * one(*cut)
    return gain


def gaussian(own_key, dims, spread, most, pieces=(), held_as=jnp.bfloat16):
    loudness = level_of(own_key, dims, pieces, -0.22, 0.18) if pieces else 1.0
    values = jax.random.normal(own_key, dims, jnp.float32) * spread * loudness
    return jnp.minimum(jnp.maximum(values, -most), most).astype(held_as)


def setup_inputs(seed: int = 0, part: int = 0) -> dict:
    streams_of = jax.random.split(jax.random.key(seed), 4)
    part_keys = jax.random.split(jax.random.fold_in(streams_of[3], part), 4)
    keys = draw_keys(jax.random.fold_in(jax.random.fold_in(streams_of[3], part), 71), part)
    values = gaussian(part_keys[1], (CONTEXT, D), 1.0, 6.0, ((0, 16),))
    queries = draw_queries(jax.random.fold_in(jax.random.fold_in(streams_of[3], part), 71), part)
    return dict(keys=keys, values=values, queries=queries)


def reference(keys, values, queries):
    scale = 1.0 / math.sqrt(HEAD_DIM)
    layer_outs = []
    for layer in range(LAYERS):
        query_layer = queries[layer]

        def one_head(head):
            start = head * HEAD_DIM
            q_head = lax.dynamic_slice_in_dim(query_layer, start, HEAD_DIM, 1)
            k_head = lax.dynamic_slice_in_dim(keys, start, HEAD_DIM, 1)
            v_head = lax.dynamic_slice_in_dim(values, start, HEAD_DIM, 1)
            scores = lax.dot_general(q_head, k_head, (((1,), (1,)), ((), ())), preferred_element_type=jnp.float32) * scale
            peak = lax.optimization_barrier(jnp.max(scores, axis=1))
            expo = jnp.exp(scores - peak[:, None])
            total = lax.optimization_barrier(jnp.sum(expo, axis=1))
            summed = jnp.dot(expo.astype(jnp.bfloat16), v_head, preferred_element_type=jnp.float32)
            return (summed / total[:, None]).astype(jnp.bfloat16)
        per_head = lax.map(one_head, jnp.arange(HEADS, dtype=jnp.int32))
        layer_outs.append(jnp.transpose(per_head, (1, 0, 2)).reshape(QUERY_TOKENS, D))
    return jnp.stack(layer_outs)
```

```python
import functools
import math

import jax
import jax.numpy as jnp
from jax import lax
from jax.experimental import pallas as pl
from jax.experimental.pallas import tpu as pltpu
from jax.sharding import PartitionSpec as P

HEAD_DIM = 128
GROUPS = 8
CORES = 2
MESH = pl.DeviceIdType.MESH
ROW_CHUNK = 128


def attend_kernel(chips, heads, k_ref, v_ref, q_ref, out_ref, kv, qs, res, kv_send, kv_recv, q_send, q_recv,
                  fwd_send, fwd_recv, o_send, o_recv):
    rows = k_ref.shape[0]
    toks = q_ref.shape[1]
    group_width = heads * HEAD_DIM
    half = chips * rows
    scale = 1.0 / math.sqrt(HEAD_DIM)
    rep = lax.axis_index("rep")
    me = lax.axis_index("seq")
    chip = lax.div(me, CORES)
    core = lax.rem(me, CORES)
    partner = me + 1 - 2 * core

    def other(mask):
        total = 0
        for bit in range(chips.bit_length() - 1):
            mine = lax.rem(lax.div(chip, 1 << bit), 2)
            total = total + ((1 - mine) if (mask >> bit) & 1 else mine) * (1 << bit)
        return total

    masks = tuple(range(chips - 1, 0, -1))
    others = [other(mask) for mask in masks]

    def remote(src, dst, send, recv, target):
        return pltpu.make_async_remote_copy(
            src_ref=src, dst_ref=dst, send_sem=send, recv_sem=recv, device_id=(rep, target), device_id_type=MESH
        )

    def columns(owner, head):
        return pl.ds(pl.multiple_of(owner * group_width + head * HEAD_DIM, HEAD_DIM), HEAD_DIM)

    barrier = pltpu.get_barrier_semaphore()
    pl.semaphore_signal(barrier, inc=1, device_id=(rep, partner), device_id_type=MESH)
    for dest in others:
        for side in range(CORES):
            pl.semaphore_signal(barrier, inc=1, device_id=(rep, CORES * dest + side), device_id_type=MESH)
    pl.semaphore_wait(barrier, CORES * chips - 1)

    my_rows = pl.ds(pl.multiple_of(chip * rows, rows), rows)
    my_toks = pl.ds(pl.multiple_of(me * toks, toks), toks)

    def send_head(head, carry):
        for dest in others:
            cols = columns(dest, head)
            remote(k_ref.at[:, cols], kv.at[head, 0, my_rows], kv_send, kv_recv.at[head], CORES * dest + core).start()
            remote(v_ref.at[:, cols], kv.at[head, 1, my_rows], kv_send, kv_recv.at[head], CORES * dest + core).start()
            for side in range(CORES):
                remote(q_ref.at[side, :, cols], qs.at[head, my_toks], q_send, q_recv.at[head], CORES * dest + side).start()
        cols = columns(chip, head)
        pltpu.make_async_copy(k_ref.at[:, cols], kv.at[head, 0, my_rows], kv_recv.at[head]).start()
        pltpu.make_async_copy(v_ref.at[:, cols], kv.at[head, 1, my_rows], kv_recv.at[head]).start()
        pltpu.make_async_copy(q_ref.at[core, :, cols], qs.at[head, my_toks], q_recv.at[head]).start()
        remote(q_ref.at[1 - core, :, cols], qs.at[head, my_toks], q_send, q_recv.at[head], partner).start()
        return carry

    lax.fori_loop(0, heads, send_head, 0)

    def attend(head, carry):
        direct = kv.at[head, :, pl.ds(0, half)]
        passed = kv.at[head, :, pl.ds(half, half)]
        pltpu.make_async_copy(direct, direct, kv_recv.at[head]).wait()
        forward = remote(direct, passed, fwd_send.at[head], fwd_recv.at[head], partner)
        forward.start()
        pltpu.make_async_copy(qs.at[head], qs.at[head], q_recv.at[head]).wait()
        forward.wait()
        for start in range(0, qs.shape[1], ROW_CHUNK):
            scores = lax.dot_general(
                qs[head, start:start + ROW_CHUNK], kv[head, 0], (((1,), (1,)), ((), ())),
                preferred_element_type=jnp.float32,
            )
            peak = jnp.max(scores, axis=1, keepdims=True)
            expo = jnp.exp((scores - peak) * scale)
            total = jnp.sum(expo, axis=1, keepdims=True)
            summed = jnp.dot(expo.astype(jnp.bfloat16), kv[head, 1], preferred_element_type=jnp.float32)
            res[head, start:start + ROW_CHUNK] = (summed / total).astype(jnp.bfloat16)
        cols = columns(chip, head)

        def block(device):
            return res.at[head, pl.ds(pl.multiple_of(device * toks, toks), toks)]

        place = out_ref.at[core, :, cols]
        for dest in others:
            for side in range(CORES):
                device = CORES * dest + side
                remote(block(device), place, o_send, o_recv, device).start()
        remote(block(partner), place, o_send, o_recv, partner).start()
        pltpu.make_async_copy(block(me), place, o_recv).start()
        return carry

    lax.fori_loop(0, heads, attend, 0)

    pltpu.make_async_copy(out_ref, out_ref, o_recv).wait()
    both = kv.at[:, :, pl.ds(0, (chips - 1) * rows)]
    pltpu.make_async_copy(both, both, kv_send).wait()
    most = qs.at[:, pl.ds(0, (CORES * chips - 1) * toks)]
    pltpu.make_async_copy(most, most, q_send).wait()
    pltpu.make_async_copy(most, most, o_send).wait()


def by_heads(keys, values, queries):
    nseq = lax.axis_size("seq")
    chips = nseq // CORES
    rows, width = keys.shape
    _, toks, _ = queries.shape
    heads = width // HEAD_DIM // chips
    any_space = pl.BlockSpec(memory_space=pl.ANY)
    dma = pltpu.SemaphoreType.DMA
    return pl.pallas_call(
        functools.partial(attend_kernel, chips, heads),
        out_shape=jax.ShapeDtypeStruct(queries.shape, jnp.bfloat16),
        in_specs=[any_space] * 3,
        out_specs=any_space,
        scratch_shapes=[
            pltpu.VMEM((heads, 2, nseq * rows, HEAD_DIM), jnp.bfloat16),
            pltpu.VMEM((heads, nseq * toks, HEAD_DIM), jnp.bfloat16),
            pltpu.VMEM((heads, nseq * toks, HEAD_DIM), jnp.bfloat16),
            dma, dma((heads,)), dma, dma((heads,)),
            dma((heads,)), dma((heads,)), dma, dma,
        ],
        compiler_params=pltpu.CompilerParams(collective_id=0, has_side_effects=True),
    )(keys, values, queries)


def by_groups(keys, values, queries):
    nseq = lax.axis_size("seq")
    blocks = nseq // GROUPS
    ctx_rows, width = keys.shape
    group_width = width // GROUPS
    heads_group = group_width // HEAD_DIM
    layers, tok_rows, _ = queries.shape
    query_total = tok_rows * nseq
    scale = 1.0 / math.sqrt(HEAD_DIM)

    def arrange(local_block):
        return local_block.reshape(ctx_rows // blocks, nseq, group_width)

    def by_source(array):
        return array.reshape((array.shape[0], blocks, GROUPS) + array.shape[2:])

    moved_keys, moved_values = (
        lax.all_to_all(arrange(keys), "seq", split_axis=1, concat_axis=1, tiled=True),
        lax.all_to_all(arrange(values), "seq", split_axis=1, concat_axis=1, tiled=True),
    )
    moved_keys = moved_keys.reshape(-1, group_width)
    moved_values = moved_values.reshape(-1, group_width)
    layer_outs = []
    for layer in range(layers):
        local_query = queries[layer]
        per_group = local_query.reshape(tok_rows, GROUPS, group_width)
        received = lax.all_to_all(
            jnp.broadcast_to(per_group[:, None], (tok_rows, blocks, GROUPS, group_width)).reshape(
                tok_rows, nseq, group_width
            ),
            "seq",
            split_axis=1,
            concat_axis=0,
            tiled=True,
        )
        own_block = received.reshape(query_total, group_width)

        def one_head(head):
            start = head * HEAD_DIM
            q_head = lax.dynamic_slice_in_dim(own_block, start, HEAD_DIM, 1)
            k_head = lax.dynamic_slice_in_dim(moved_keys, start, HEAD_DIM, 1)
            v_head = lax.dynamic_slice_in_dim(moved_values, start, HEAD_DIM, 1)
            scores = (
                lax.dot_general(
                    q_head, k_head, (((1,), (1,)), ((), ())), preferred_element_type=jnp.float32
                )
                * scale
            )
            peak = jnp.max(scores, axis=1)
            expo = jnp.exp(scores - peak[:, None])
            total = jnp.sum(expo, axis=1)
            summed = jnp.dot(expo.astype(jnp.bfloat16), v_head, preferred_element_type=jnp.float32)
            return (summed, peak, total)

        summed, peak, total = lax.map(one_head, jnp.arange(heads_group, dtype=jnp.int32))
        shaped = (
            summed.reshape(heads_group, nseq, tok_rows, HEAD_DIM),
            peak.reshape(heads_group, nseq, tok_rows),
            total.reshape(heads_group, nseq, tok_rows),
        )
        combine_summed = lax.all_to_all(shaped[0], "seq", split_axis=1, concat_axis=1, tiled=True)
        combine_peak = lax.all_to_all(shaped[1], "seq", split_axis=1, concat_axis=1, tiled=True)
        combine_total = lax.all_to_all(shaped[2], "seq", split_axis=1, concat_axis=1, tiled=True)
        rows = combine_peak.shape[2]
        summed_s = by_source(combine_summed)
        peak_s = by_source(combine_peak)
        total_s = by_source(combine_total)
        highest = jnp.max(peak_s, axis=1)
        factor = jnp.exp(peak_s - highest[:, None])
        denom = jnp.sum(factor * total_s, axis=1)
        numer = jnp.sum(factor[..., None] * summed_s, axis=1)
        result = numer / denom[..., None]
        result = jnp.transpose(result, (2, 1, 0, 3)).reshape(rows, GROUPS * heads_group * HEAD_DIM)
        mixed = result.astype(jnp.bfloat16)
        layer_outs.append(mixed)
    return jnp.stack(layer_outs)


def local(keys, values, queries):
    chips = lax.axis_size("seq") // CORES
    heads = keys.shape[1] // HEAD_DIM
    whole_heads = heads % chips == 0 and chips & (chips - 1) == 0
    if whole_heads and queries.shape[0] == CORES and queries.shape[1] % 16 == 0:
        return by_heads(keys, values, queries)
    return by_groups(keys, values, queries)


def solution(mesh):
    return jax.shard_map(
        local,
        mesh=mesh,
        in_specs=(P(("rep", "seq"), None), P(("rep", "seq"), None), P(None, ("rep", "seq"), None)),
        out_specs=P(None, ("rep", "seq"), None),
        check_vma=False,
    )
```

```python
import functools
import math

import jax
import jax.numpy as jnp
from jax import lax
from jax.experimental import pallas as pl
from jax.experimental.pallas import tpu as pltpu
from jax.sharding import PartitionSpec as P

HEAD_DIM = 128
GROUPS = 8
CORES = 2
MESH = pl.DeviceIdType.MESH
ROW_CHUNK = 128


def attend_kernel(chips, heads, k_ref, v_ref, q_ref, out_ref, kv, qs, res, kv_send, kv_recv, q_send, q_recv,
                  fwd_send, fwd_recv, o_send, o_recv):
    rows = k_ref.shape[0]
    toks = q_ref.shape[1]
    group_width = heads * HEAD_DIM
    half = chips * rows
    scale = 1.0 / math.sqrt(HEAD_DIM)
    rep = lax.axis_index("rep")
    me = lax.axis_index("seq")
    chip = lax.div(me, CORES)
    core = lax.rem(me, CORES)
    partner = me + 1 - 2 * core

    def other(mask):
        total = 0
        for bit in range(chips.bit_length() - 1):
            mine = lax.rem(lax.div(chip, 1 << bit), 2)
            total = total + ((1 - mine) if (mask >> bit) & 1 else mine) * (1 << bit)
        return total

    masks = tuple(range(chips - 1, 0, -1))
    others = [other(mask) for mask in masks]

    def remote(src, dst, send, recv, target):
        return pltpu.make_async_remote_copy(
            src_ref=src, dst_ref=dst, send_sem=send, recv_sem=recv, device_id=(rep, target), device_id_type=MESH
        )

    def columns(owner, head):
        return pl.ds(pl.multiple_of(owner * group_width + head * HEAD_DIM, HEAD_DIM), HEAD_DIM)

    barrier = pltpu.get_barrier_semaphore()
    pl.semaphore_signal(barrier, inc=1, device_id=(rep, partner), device_id_type=MESH)
    for dest in others:
        for side in range(CORES):
            pl.semaphore_signal(barrier, inc=1, device_id=(rep, CORES * dest + side), device_id_type=MESH)
    pl.semaphore_wait(barrier, CORES * chips - 1)

    my_rows = pl.ds(pl.multiple_of(chip * rows, rows), rows)
    my_toks = pl.ds(pl.multiple_of(me * toks, toks), toks)

    far = [other(mask) for mask in masks if mask >= 4]
    close = [other(mask) for mask in masks if mask < 4]

    def send_to(dest, head):
        cols = columns(dest, head)
        remote(k_ref.at[:, cols], kv.at[head, 0, my_rows], kv_send, kv_recv.at[head], CORES * dest + core).start()
        remote(v_ref.at[:, cols], kv.at[head, 1, my_rows], kv_send, kv_recv.at[head], CORES * dest + core).start()
        for side in range(CORES):
            remote(q_ref.at[side, :, cols], qs.at[head, my_toks], q_send, q_recv.at[head], CORES * dest + side).start()

    def keep(head):
        cols = columns(chip, head)
        pltpu.make_async_copy(k_ref.at[:, cols], kv.at[head, 0, my_rows], kv_recv.at[head]).start()
        pltpu.make_async_copy(v_ref.at[:, cols], kv.at[head, 1, my_rows], kv_recv.at[head]).start()
        pltpu.make_async_copy(q_ref.at[core, :, cols], qs.at[head, my_toks], q_recv.at[head]).start()
        remote(q_ref.at[1 - core, :, cols], qs.at[head, my_toks], q_send, q_recv.at[head], partner).start()

    def send_all(dests):
        def send_head(head, carry):
            for dest in dests:
                send_to(dest, head)
            return carry

        lax.fori_loop(0, heads, send_head, 0)

    def keep_head(head, carry):
        keep(head)
        return carry

    send_all(far)
    send_all(close)
    lax.fori_loop(0, heads, keep_head, 0)

    def attend(head, carry):
        direct = kv.at[head, :, pl.ds(0, half)]
        passed = kv.at[head, :, pl.ds(half, half)]
        pltpu.make_async_copy(direct, direct, kv_recv.at[head]).wait()
        forward = remote(direct, passed, fwd_send.at[head], fwd_recv.at[head], partner)
        forward.start()
        pltpu.make_async_copy(qs.at[head], qs.at[head], q_recv.at[head]).wait()
        forward.wait()
        for start in range(0, qs.shape[1], ROW_CHUNK):
            scores = lax.dot_general(
                qs[head, start:start + ROW_CHUNK], kv[head, 0], (((1,), (1,)), ((), ())),
                preferred_element_type=jnp.float32,
            )
            peak = jnp.max(scores, axis=1, keepdims=True)
            expo = jnp.exp((scores - peak) * scale)
            total = jnp.sum(expo, axis=1, keepdims=True)
            summed = jnp.dot(expo.astype(jnp.bfloat16), kv[head, 1], preferred_element_type=jnp.float32)
            res[head, start:start + ROW_CHUNK] = (summed / total).astype(jnp.bfloat16)
        cols = columns(chip, head)

        def block(device):
            return res.at[head, pl.ds(pl.multiple_of(device * toks, toks), toks)]

        place = out_ref.at[core, :, cols]
        for dest in others:
            for side in range(CORES):
                device = CORES * dest + side
                remote(block(device), place, o_send, o_recv, device).start()
        remote(block(partner), place, o_send, o_recv, partner).start()
        pltpu.make_async_copy(block(me), place, o_recv).start()
        return carry

    lax.fori_loop(0, heads, attend, 0)

    pltpu.make_async_copy(out_ref, out_ref, o_recv).wait()
    both = kv.at[:, :, pl.ds(0, (chips - 1) * rows)]
    pltpu.make_async_copy(both, both, kv_send).wait()
    most = qs.at[:, pl.ds(0, (CORES * chips - 1) * toks)]
    pltpu.make_async_copy(most, most, q_send).wait()
    pltpu.make_async_copy(most, most, o_send).wait()


def by_heads(keys, values, queries):
    nseq = lax.axis_size("seq")
    chips = nseq // CORES
    rows, width = keys.shape
    _, toks, _ = queries.shape
    heads = width // HEAD_DIM // chips
    any_space = pl.BlockSpec(memory_space=pl.ANY)
    dma = pltpu.SemaphoreType.DMA
    return pl.pallas_call(
        functools.partial(attend_kernel, chips, heads),
        out_shape=pltpu.VMEM(queries.shape, jnp.bfloat16),
        in_specs=[any_space] * 3,
        out_specs=pl.BlockSpec(memory_space=pltpu.VMEM),
        scratch_shapes=[
            pltpu.VMEM((heads, 2, nseq * rows, HEAD_DIM), jnp.bfloat16),
            pltpu.VMEM((heads, nseq * toks, HEAD_DIM), jnp.bfloat16),
            pltpu.VMEM((heads, nseq * toks, HEAD_DIM), jnp.bfloat16),
            dma, dma((heads,)), dma, dma((heads,)),
            dma((heads,)), dma((heads,)), dma, dma,
        ],
        compiler_params=pltpu.CompilerParams(collective_id=0, has_side_effects=True),
    )(keys, values, queries)


def by_groups(keys, values, queries):
    nseq = lax.axis_size("seq")
    blocks = nseq // GROUPS
    ctx_rows, width = keys.shape
    group_width = width // GROUPS
    heads_group = group_width // HEAD_DIM
    layers, tok_rows, _ = queries.shape
    query_total = tok_rows * nseq
    scale = 1.0 / math.sqrt(HEAD_DIM)

    def arrange(local_block):
        return local_block.reshape(ctx_rows // blocks, nseq, group_width)

    def by_source(array):
        return array.reshape((array.shape[0], blocks, GROUPS) + array.shape[2:])

    moved_keys, moved_values = (
        lax.all_to_all(arrange(keys), "seq", split_axis=1, concat_axis=1, tiled=True),
        lax.all_to_all(arrange(values), "seq", split_axis=1, concat_axis=1, tiled=True),
    )
    moved_keys = moved_keys.reshape(-1, group_width)
    moved_values = moved_values.reshape(-1, group_width)
    layer_outs = []
    for layer in range(layers):
        local_query = queries[layer]
        per_group = local_query.reshape(tok_rows, GROUPS, group_width)
        received = lax.all_to_all(
            jnp.broadcast_to(per_group[:, None], (tok_rows, blocks, GROUPS, group_width)).reshape(
                tok_rows, nseq, group_width
            ),
            "seq",
            split_axis=1,
            concat_axis=0,
            tiled=True,
        )
        own_block = received.reshape(query_total, group_width)

        def one_head(head):
            start = head * HEAD_DIM
            q_head = lax.dynamic_slice_in_dim(own_block, start, HEAD_DIM, 1)
            k_head = lax.dynamic_slice_in_dim(moved_keys, start, HEAD_DIM, 1)
            v_head = lax.dynamic_slice_in_dim(moved_values, start, HEAD_DIM, 1)
            scores = (
                lax.dot_general(
                    q_head, k_head, (((1,), (1,)), ((), ())), preferred_element_type=jnp.float32
                )
                * scale
            )
            peak = jnp.max(scores, axis=1)
            expo = jnp.exp(scores - peak[:, None])
            total = jnp.sum(expo, axis=1)
            summed = jnp.dot(expo.astype(jnp.bfloat16), v_head, preferred_element_type=jnp.float32)
            return (summed, peak, total)

        summed, peak, total = lax.map(one_head, jnp.arange(heads_group, dtype=jnp.int32))
        shaped = (
            summed.reshape(heads_group, nseq, tok_rows, HEAD_DIM),
            peak.reshape(heads_group, nseq, tok_rows),
            total.reshape(heads_group, nseq, tok_rows),
        )
        combine_summed = lax.all_to_all(shaped[0], "seq", split_axis=1, concat_axis=1, tiled=True)
        combine_peak = lax.all_to_all(shaped[1], "seq", split_axis=1, concat_axis=1, tiled=True)
        combine_total = lax.all_to_all(shaped[2], "seq", split_axis=1, concat_axis=1, tiled=True)
        rows = combine_peak.shape[2]
        summed_s = by_source(combine_summed)
        peak_s = by_source(combine_peak)
        total_s = by_source(combine_total)
        highest = jnp.max(peak_s, axis=1)
        factor = jnp.exp(peak_s - highest[:, None])
        denom = jnp.sum(factor * total_s, axis=1)
        numer = jnp.sum(factor[..., None] * summed_s, axis=1)
        result = numer / denom[..., None]
        result = jnp.transpose(result, (2, 1, 0, 3)).reshape(rows, GROUPS * heads_group * HEAD_DIM)
        mixed = result.astype(jnp.bfloat16)
        layer_outs.append(mixed)
    return jnp.stack(layer_outs)


def local(keys, values, queries):
    chips = lax.axis_size("seq") // CORES
    heads = keys.shape[1] // HEAD_DIM
    if chips == 8 and heads % chips == 0 and queries.shape[0] == CORES and queries.shape[1] % 16 == 0:
        return by_heads(keys, values, queries)
    return by_groups(keys, values, queries)


def solution(mesh):
    return jax.shard_map(
        local,
        mesh=mesh,
        in_specs=(P(("rep", "seq"), None), P(("rep", "seq"), None), P(None, ("rep", "seq"), None)),
        out_specs=P(None, ("rep", "seq"), None),
        check_vma=False,
    )
```

```python
import functools
import math

import jax
import jax.numpy as jnp
from jax import lax
from jax.experimental import pallas as pl
from jax.experimental.pallas import tpu as pltpu
from jax.sharding import PartitionSpec as P

HEAD_DIM = 128
GROUPS = 8
CORES = 2
MESH = pl.DeviceIdType.MESH


def attend_kernel(chips, heads, k_ref, v_ref, q_ref, out_ref, kv, qs, res, kv_send, kv_recv, q_send, q_recv,
                  fwd_send, fwd_recv, o_send, o_recv):
    rows = k_ref.shape[0]
    toks = q_ref.shape[1]
    group_width = heads * HEAD_DIM
    half = chips * rows
    scale = 1.0 / math.sqrt(HEAD_DIM)
    rep = lax.axis_index("rep")
    me = lax.axis_index("seq")
    chip = lax.div(me, CORES)
    core = lax.rem(me, CORES)
    partner = me + 1 - 2 * core

    def other(mask):
        total = 0
        for bit in range(chips.bit_length() - 1):
            mine = lax.rem(lax.div(chip, 1 << bit), 2)
            total = total + ((1 - mine) if (mask >> bit) & 1 else mine) * (1 << bit)
        return total

    masks = tuple(range(chips - 1, 0, -1))
    others = [other(mask) for mask in masks]

    def remote(src, dst, send, recv, target):
        return pltpu.make_async_remote_copy(
            src_ref=src, dst_ref=dst, send_sem=send, recv_sem=recv, device_id=(rep, target), device_id_type=MESH
        )

    def columns(owner, head):
        return pl.ds(pl.multiple_of(owner * group_width + head * HEAD_DIM, HEAD_DIM), HEAD_DIM)

    barrier = pltpu.get_barrier_semaphore()
    pl.semaphore_signal(barrier, inc=1, device_id=(rep, partner), device_id_type=MESH)
    for dest in others:
        for side in range(CORES):
            pl.semaphore_signal(barrier, inc=1, device_id=(rep, CORES * dest + side), device_id_type=MESH)
    pl.semaphore_wait(barrier, CORES * chips - 1)

    my_rows = pl.ds(pl.multiple_of(chip * rows, rows), rows)
    my_toks = pl.ds(pl.multiple_of(me * toks, toks), toks)

    far = [other(mask) for mask in masks if mask >= 4]
    close = [other(mask) for mask in masks if mask < 4]

    def send_to(dest, head):
        cols = columns(dest, head)
        remote(k_ref.at[:, cols], kv.at[head, 0, my_rows], kv_send, kv_recv.at[head], CORES * dest + core).start()
        remote(v_ref.at[:, cols], kv.at[head, 1, my_rows], kv_send, kv_recv.at[head], CORES * dest + core).start()
        for side in range(CORES):
            remote(q_ref.at[side, :, cols], qs.at[head, my_toks], q_send, q_recv.at[head], CORES * dest + side).start()

    def keep(head):
        cols = columns(chip, head)
        pltpu.make_async_copy(k_ref.at[:, cols], kv.at[head, 0, my_rows], kv_recv.at[head]).start()
        pltpu.make_async_copy(v_ref.at[:, cols], kv.at[head, 1, my_rows], kv_recv.at[head]).start()
        pltpu.make_async_copy(q_ref.at[core, :, cols], qs.at[head, my_toks], q_recv.at[head]).start()
        remote(q_ref.at[1 - core, :, cols], qs.at[head, my_toks], q_send, q_recv.at[head], partner).start()

    def send_all(dests):
        def send_head(head, carry):
            for dest in dests:
                send_to(dest, head)
            return carry

        lax.fori_loop(0, heads, send_head, 0)

    def keep_head(head, carry):
        keep(head)
        return carry

    send_all(far)
    send_all(close)
    lax.fori_loop(0, heads, keep_head, 0)

    def attend(head, carry):
        direct = kv.at[head, :, pl.ds(0, half)]
        passed = kv.at[head, :, pl.ds(half, half)]
        pltpu.make_async_copy(direct, direct, kv_recv.at[head]).wait()
        forward = remote(direct, passed, fwd_send.at[head], fwd_recv.at[head], partner)
        forward.start()
        pltpu.make_async_copy(qs.at[head], qs.at[head], q_recv.at[head]).wait()
        forward.wait()
        place = out_ref.at[core, :, columns(chip, head)]
        chunk = 2 * CORES * toks

        def block(device):
            return res.at[head, pl.ds(pl.multiple_of(device * toks, toks), toks)]

        for pair in range(chips // 2 - 1, -1, -1):
            part = pl.ds(pl.multiple_of(lax.div(other(2 * pair), 2) * chunk, chunk), chunk)
            scores = lax.dot_general(
                qs[head, part], kv[head, 0], (((1,), (1,)), ((), ())), preferred_element_type=jnp.float32
            )
            peak = jnp.max(scores, axis=1, keepdims=True)
            expo = jnp.exp((scores - peak) * scale)
            total = jnp.sum(expo, axis=1, keepdims=True)
            summed = jnp.dot(expo.astype(jnp.bfloat16), kv[head, 1], preferred_element_type=jnp.float32)
            res[head, part] = (summed / total).astype(jnp.bfloat16)
            for mask in (2 * pair, 2 * pair + 1):
                if mask:
                    for side in range(CORES):
                        device = CORES * other(mask) + side
                        remote(block(device), place, o_send, o_recv, device).start()
        remote(block(partner), place, o_send, o_recv, partner).start()
        pltpu.make_async_copy(block(me), place, o_recv).start()
        return carry

    lax.fori_loop(0, heads, attend, 0)

    pltpu.make_async_copy(out_ref, out_ref, o_recv).wait()
    both = kv.at[:, :, pl.ds(0, (chips - 1) * rows)]
    pltpu.make_async_copy(both, both, kv_send).wait()
    most = qs.at[:, pl.ds(0, (CORES * chips - 1) * toks)]
    pltpu.make_async_copy(most, most, q_send).wait()
    pltpu.make_async_copy(most, most, o_send).wait()


def by_heads(keys, values, queries):
    nseq = lax.axis_size("seq")
    chips = nseq // CORES
    rows, width = keys.shape
    _, toks, _ = queries.shape
    heads = width // HEAD_DIM // chips
    any_space = pl.BlockSpec(memory_space=pl.ANY)
    dma = pltpu.SemaphoreType.DMA
    return pl.pallas_call(
        functools.partial(attend_kernel, chips, heads),
        out_shape=pltpu.VMEM(queries.shape, jnp.bfloat16),
        in_specs=[any_space] * 3,
        out_specs=pl.BlockSpec(memory_space=pltpu.VMEM),
        scratch_shapes=[
            pltpu.VMEM((heads, 2, nseq * rows, HEAD_DIM), jnp.bfloat16),
            pltpu.VMEM((heads, nseq * toks, HEAD_DIM), jnp.bfloat16),
            pltpu.VMEM((heads, nseq * toks, HEAD_DIM), jnp.bfloat16),
            dma, dma((heads,)), dma, dma((heads,)),
            dma((heads,)), dma((heads,)), dma, dma,
        ],
        compiler_params=pltpu.CompilerParams(collective_id=0, has_side_effects=True),
    )(keys, values, queries)


def by_groups(keys, values, queries):
    nseq = lax.axis_size("seq")
    blocks = nseq // GROUPS
    ctx_rows, width = keys.shape
    group_width = width // GROUPS
    heads_group = group_width // HEAD_DIM
    layers, tok_rows, _ = queries.shape
    query_total = tok_rows * nseq
    scale = 1.0 / math.sqrt(HEAD_DIM)

    def arrange(local_block):
        return local_block.reshape(ctx_rows // blocks, nseq, group_width)

    def by_source(array):
        return array.reshape((array.shape[0], blocks, GROUPS) + array.shape[2:])

    moved_keys, moved_values = (
        lax.all_to_all(arrange(keys), "seq", split_axis=1, concat_axis=1, tiled=True),
        lax.all_to_all(arrange(values), "seq", split_axis=1, concat_axis=1, tiled=True),
    )
    moved_keys = moved_keys.reshape(-1, group_width)
    moved_values = moved_values.reshape(-1, group_width)
    layer_outs = []
    for layer in range(layers):
        local_query = queries[layer]
        per_group = local_query.reshape(tok_rows, GROUPS, group_width)
        received = lax.all_to_all(
            jnp.broadcast_to(per_group[:, None], (tok_rows, blocks, GROUPS, group_width)).reshape(
                tok_rows, nseq, group_width
            ),
            "seq",
            split_axis=1,
            concat_axis=0,
            tiled=True,
        )
        own_block = received.reshape(query_total, group_width)

        def one_head(head):
            start = head * HEAD_DIM
            q_head = lax.dynamic_slice_in_dim(own_block, start, HEAD_DIM, 1)
            k_head = lax.dynamic_slice_in_dim(moved_keys, start, HEAD_DIM, 1)
            v_head = lax.dynamic_slice_in_dim(moved_values, start, HEAD_DIM, 1)
            scores = (
                lax.dot_general(
                    q_head, k_head, (((1,), (1,)), ((), ())), preferred_element_type=jnp.float32
                )
                * scale
            )
            peak = jnp.max(scores, axis=1)
            expo = jnp.exp(scores - peak[:, None])
            total = jnp.sum(expo, axis=1)
            summed = jnp.dot(expo.astype(jnp.bfloat16), v_head, preferred_element_type=jnp.float32)
            return (summed, peak, total)

        summed, peak, total = lax.map(one_head, jnp.arange(heads_group, dtype=jnp.int32))
        shaped = (
            summed.reshape(heads_group, nseq, tok_rows, HEAD_DIM),
            peak.reshape(heads_group, nseq, tok_rows),
            total.reshape(heads_group, nseq, tok_rows),
        )
        combine_summed = lax.all_to_all(shaped[0], "seq", split_axis=1, concat_axis=1, tiled=True)
        combine_peak = lax.all_to_all(shaped[1], "seq", split_axis=1, concat_axis=1, tiled=True)
        combine_total = lax.all_to_all(shaped[2], "seq", split_axis=1, concat_axis=1, tiled=True)
        rows = combine_peak.shape[2]
        summed_s = by_source(combine_summed)
        peak_s = by_source(combine_peak)
        total_s = by_source(combine_total)
        highest = jnp.max(peak_s, axis=1)
        factor = jnp.exp(peak_s - highest[:, None])
        denom = jnp.sum(factor * total_s, axis=1)
        numer = jnp.sum(factor[..., None] * summed_s, axis=1)
        result = numer / denom[..., None]
        result = jnp.transpose(result, (2, 1, 0, 3)).reshape(rows, GROUPS * heads_group * HEAD_DIM)
        mixed = result.astype(jnp.bfloat16)
        layer_outs.append(mixed)
    return jnp.stack(layer_outs)


def local(keys, values, queries):
    chips = lax.axis_size("seq") // CORES
    heads = keys.shape[1] // HEAD_DIM
    if chips == 8 and heads % chips == 0 and queries.shape[0] == CORES and queries.shape[1] % 16 == 0:
        return by_heads(keys, values, queries)
    return by_groups(keys, values, queries)


def solution(mesh):
    return jax.shard_map(
        local,
        mesh=mesh,
        in_specs=(P(("rep", "seq"), None), P(("rep", "seq"), None), P(None, ("rep", "seq"), None)),
        out_specs=P(None, ("rep", "seq"), None),
        check_vma=False,
    )
```
